32 devices in a mesh: ctx: 8 (over z, x), head: 4 (over y, core).
Axes of the slice: x: 2, y: 2, z: 4, core: 2. Of those that a mesh axis runs over, the one named last changes fastest.
Arguments:
- qkv: bfloat16 [4096, 12288], P(('ctx', 'head')), may hold values from -26 to 26
- grad_out: bfloat16 [4096, 4096], P(('ctx', 'head')), may hold values from -6 to 6
- key_lists: int32 [32, 4], P('ctx'), may hold values from 0 to 31, as said below
- live_counts: int32 [32], P('ctx'), may hold values from 1 to 4
Outputs:
- grad_qkv: bfloat16 [4096, 12288], P(('ctx', 'head'))
The draws below stay inside these ranges and needn't reach their ends.
Inputs may be any that keep to these rules, and one draw needn't show every extreme that they name: `key_lists`: each entry names a block whose index of ctx is within 2 of its query block's and which is not within one block of its query block; the 4 entries of a row differ. Over all 4 entries of all rows (live or not) of one index of ctx, the blocks named on any other index of ctx are at most 2 of its blocks, and this is reached.
All inputs are finite; a program needn't handle non-finite values.
Results may differ from the reference program's by a relative error of at most 0.008.
Values may be sent and summed in bfloat16 or wider, within the bound.
A program may use at most 192 MiB of HBM per device.

```python
import jax
import jax.numpy as jnp
from jax import lax

HEADS = 32
HD = 128
BLK = 128
SEARCHER_TILES = 4
DRAWN_TARGET_SET = 4
SPAN = 2
NAMED_TILE_LIMIT = 2
NB = 32
TOKENS = 4096


def draw_qkv(key, part):
    shape = (TOKENS, HEADS, 3, HD)
    base = jnp.clip(jax.random.normal(key, shape, jnp.float32), -6.0, 6.0)
    return base.reshape(TOKENS, HEADS * 3 * HD).astype(jnp.bfloat16)


def draw_key_lists(key, part):
    shard_total = NB // SEARCHER_TILES
    neighbourhood_halfwidth = 2 * SPAN
    sides = jnp.array([side for side in range(-SPAN, SPAN + 1) if side != 0], dtype=jnp.int32)

    def pick_allowed(subkey):
        return jax.random.permutation(subkey, SEARCHER_TILES)[:NAMED_TILE_LIMIT].astype(jnp.int32)
    allowed = jax.vmap(pick_allowed)(jax.random.split(jax.random.fold_in(key, 11), shard_total * neighbourhood_halfwidth))
    allowed = allowed.reshape(shard_total, neighbourhood_halfwidth, NAMED_TILE_LIMIT)
    tile_ordinals = jnp.arange(NB, dtype=jnp.int32)
    shard_of = tile_ordinals // SEARCHER_TILES
    own_blocks = shard_of[:, None] * SEARCHER_TILES + jnp.arange(SEARCHER_TILES, dtype=jnp.int32)[None, :]
    neighbour = shard_of[:, None] + sides[None, :]
    picked = allowed[shard_of]
    far_blocks = (neighbour[:, :, None] * SEARCHER_TILES + picked).reshape(NB, neighbourhood_halfwidth * NAMED_TILE_LIMIT)
    far_ok = jnp.repeat((neighbour >= 0) & (neighbour < shard_total), NAMED_TILE_LIMIT, axis=1)
    candidates = jnp.concatenate([own_blocks, far_blocks], axis=1)
    usable = jnp.concatenate([jnp.ones((NB, SEARCHER_TILES), bool), far_ok], axis=1)
    usable = usable & (jnp.abs(candidates - tile_ordinals[:, None]) > 1)
    width_all = SEARCHER_TILES + neighbourhood_halfwidth * NAMED_TILE_LIMIT

    def row_order(subkey):
        return jax.random.permutation(subkey, width_all).astype(jnp.int32)
    orders = jax.vmap(row_order)(jax.random.split(jax.random.fold_in(key, 13), NB)) + 1
    tile_merits = jnp.where(usable, orders, 0)
    target_positions = jnp.arange(width_all, dtype=jnp.int32)
    preference_reward = jnp.where((tile_ordinals[:, None] == 0) & (target_positions[None, :] >= SEARCHER_TILES + (neighbourhood_halfwidth - 1) * NAMED_TILE_LIMIT), 1000, 0)
    sorted_tiles = lax.top_k(tile_merits + preference_reward, DRAWN_TARGET_SET)[1]
    return jnp.take_along_axis(candidates, sorted_tiles, axis=1).astype(jnp.int32)


def touch_ends(values, key, low, top_value):
    longest = values.shape.index(max(values.shape))
    spots = []
    for shift in (0, 1):
        where = [jax.random.randint(jax.random.fold_in(key, axis), (), 0, length) for axis, length in enumerate(values.shape)]
        where[longest] = (where[longest] + shift) % values.shape[longest]
        spots.append(tuple(where))
    return values.at[spots[0]].set(low).at[spots[1]].set(top_value)


def block_scale(own_key, dims, cuts, smallest, high):
    gain, own = 1.0, jax.random.fold_in(own_key, 6)
    for position, parts in cuts:
        steps = jnp.exp(jax.random.uniform(jax.random.fold_in(own, position), (parts,), jnp.float32, smallest / len(cuts), high / len(cuts)))
        gain = gain * jnp.repeat(steps, dims[position] // parts).reshape([-1 if axis == position else 1 for axis in range(len(dims))])
    return gain


def noise(key, dims, scale, reach, cuts=(), held_as=jnp.bfloat16):
    values = jax.random.normal(key, dims, jnp.float32) * scale
    if len(cuts) > 0:
        values = block_scale(key, dims, cuts, -0.22, 0.18) * values
    return jnp.clip(values, min=-reach, max=reach).astype(held_as)


def setup_inputs(seed: int = 0) -> dict:
    arg_keys = jax.random.split(jax.random.key(seed), 5)
    qkv = draw_qkv(jax.random.fold_in(arg_keys[4], 71), 0)
    grad_out = noise(arg_keys[1], (TOKENS, HEADS * HD), 1.0, 6.0, ((0, 32),))
    key_lists = draw_key_lists(jax.random.fold_in(arg_keys[4], 71), 0)
    live_counts = touch_ends(jax.random.randint(arg_keys[3], (NB,), 1, DRAWN_TARGET_SET + 1), jax.random.fold_in(arg_keys[3], 1), 1, DRAWN_TARGET_SET).astype(jnp.int32)
    return {"qkv": qkv, "grad_out": grad_out, "key_lists": key_lists, "live_counts": live_counts}


def reference(qkv, grad_out, key_lists, live_counts):
    total_blocks = key_lists.shape[0]
    scaling = HD ** -0.5
    merged = qkv.reshape(total_blocks, BLK, HEADS, 3, HD)
    queries = merged[:, :, :, 0]
    key_rows = merged[:, :, :, 1]
    value_rows = merged[:, :, :, 2]
    grads_in = grad_out.reshape(total_blocks, BLK, HEADS, HD)

    def one_block(totals, block_id):
        window = block_id - 1 + jnp.arange(3, dtype=jnp.int32)
        listed = key_lists[block_id].astype(jnp.int32)
        named = jnp.concatenate([window, listed]).astype(jnp.int32)
        usable = jnp.concatenate([(window >= 0) & (window < total_blocks), jnp.arange(DRAWN_TARGET_SET, dtype=jnp.int32) < live_counts[block_id]])
        clipped = jnp.clip(named, 0, total_blocks - 1).astype(jnp.int32)
        key_part = key_rows[clipped].astype(jnp.float32)
        value_part = value_rows[clipped].astype(jnp.float32)
        query_part = queries[block_id].astype(jnp.float32)
        grad_part = grads_in[block_id].astype(jnp.float32)
        weight = usable.astype(jnp.float32)[None, None, :, None]
        tile_merits = jnp.einsum("qhd,nkhd->hqnk", query_part, key_part) * scaling
        masked = jnp.where(weight > 0.0, tile_merits, -1.0e30)
        highest = jnp.max(masked, axis=(2, 3), keepdims=True)
        powers = jnp.exp(masked - highest) * weight
        soft_weights = powers / jnp.sum(powers, axis=(2, 3), keepdims=True)
        grad_soft = jnp.einsum("qhd,nkhd->hqnk", grad_part, value_part)
        row_delta = jnp.sum(soft_weights * grad_soft, axis=(2, 3), keepdims=True)
        grad_scores = soft_weights * (grad_soft - row_delta)
        soft_low = soft_weights.astype(jnp.bfloat16).astype(jnp.float32)
        scores_low = grad_scores.astype(jnp.bfloat16).astype(jnp.float32)
        grad_values = jnp.einsum("hqnk,qhd->nkhd", soft_low, grad_part)
        grad_keys = jnp.einsum("hqnk,qhd->nkhd", scores_low, query_part) * scaling
        grad_query = jnp.einsum("hqnk,nkhd->qhd", scores_low, key_part) * scaling
        totals = totals.at[clipped].add(jnp.stack([grad_keys, grad_values], axis=3))
        return totals, grad_query

    start_totals = jnp.zeros((total_blocks, BLK, HEADS, 2, HD), jnp.float32)
    totals, grad_query = lax.scan(one_block, start_totals, jnp.arange(total_blocks, dtype=jnp.int32))
    joined = jnp.concatenate([grad_query[:, :, :, None, :], totals], axis=3)
    return joined.astype(jnp.bfloat16).reshape(total_blocks * BLK, HEADS * 3 * HD)
```

```python
import functools

import jax
import jax.numpy as jnp
from jax import lax
from jax.experimental import pallas as pl
from jax.experimental.pallas import tpu as pltpu
from jax.sharding import Mesh, PartitionSpec as P

HD = 128
BLK = 128
TILES = 4
LISTED = 4
NAMED = 2
PAIR = 2 * TILES
EDGE = NAMED + TILES
ALL = 2 * EDGE + PAIR
SCALE = HD ** (-0.5)
CHUNKS = 2
F32 = jnp.float32
BF16 = jnp.bfloat16


def rows(block, count=1):
    start = block * BLK
    return pl.ds(start if isinstance(start, int) else pl.multiple_of(start, BLK), count * BLK)


def pack_kernel(slots, own, to_next, to_prev):
    for s in range(NAMED):
        to_next[rows(s), :] = own[rows(slots[0, s]), HD:]
        to_prev[rows(TILES + s), :] = own[rows(TILES + slots[1, s]), HD:]
    to_next[rows(NAMED, TILES), :] = own[rows(TILES, TILES), HD:]
    to_prev[rows(0, TILES), :] = own[rows(0, TILES), HD:]


def attention_kernel(places, info, own, grads, left, right, dq, own_grads, left_grads, right_grads, pairs, acc):
    pairs[rows(0, EDGE), :] = left[...]
    pairs[rows(EDGE, PAIR), :] = own[:, HD:]
    pairs[rows(EDGE + PAIR, EDGE), :] = right[...]
    acc[...] = jnp.zeros_like(acc)

    def step(i, carry):
        q = own[rows(i), :HD]
        g = grads[rows(i), :]
        zero = jnp.zeros_like(q)
        both = jnp.concatenate(
            [jnp.concatenate([q, zero], axis=1), jnp.concatenate([zero, g], axis=1)], axis=0
        )
        where = [EDGE - 1 + i + n for n in range(3)] + [places[i, j] for j in range(LISTED)]
        live = info[0, i]
        usable = [info[1, i] > 0, None, info[2, i] > 0] + [live > j for j in range(LISTED)]
        kv = jnp.concatenate([pairs[rows(p), :] for p in where], axis=0)
        products = lax.dot_general(kv, both, (((1,), (1,)), ((), ())), preferred_element_type=F32)
        scores = []
        for n, ok in enumerate(usable):
            s = products[n * BLK : (n + 1) * BLK, :HD] * SCALE
            scores.append(s if ok is None else jnp.where(ok, s, -1e30))
        scores = jnp.concatenate(scores, axis=0)
        powers = jnp.exp(scores - jnp.max(scores, axis=0, keepdims=True))
        soft = powers * (1.0 / jnp.sum(powers, axis=0, keepdims=True))
        dp = products[:, HD:]
        ds = soft * (dp - jnp.sum(soft * dp, axis=0, keepdims=True))
        ds_low = ds.astype(BF16)
        low = jnp.concatenate([ds_low, soft.astype(BF16)], axis=1)
        terms = jnp.dot(low, both, preferred_element_type=F32)
        grad_q = lax.dot_general(ds_low, kv[:, :HD], (((0,), (0,)), ((), ())), preferred_element_type=F32)
        dq[rows(i), :] = (grad_q * SCALE).astype(BF16)
        acc[rows(EDGE - 1 + i, 3), :] += terms[: 3 * BLK]
        for j in range(LISTED):
            acc[rows(where[3 + j]), :] += terms[(3 + j) * BLK : (4 + j) * BLK]
        return carry

    lax.fori_loop(0, PAIR, step, 0)
    for k, factor in ((0, SCALE), (HD, 1.0)):
        columns = slice(k, k + HD)
        own_grads[:, columns] = acc[rows(EDGE, PAIR), columns] * factor
        left_grads[:, columns] = (acc[rows(0, EDGE), columns] * factor).astype(BF16)
        right_grads[:, columns] = (acc[rows(EDGE + PAIR, EDGE), columns] * factor).astype(BF16)


def combine_kernel(slots, dq, own_grads, from_next, from_prev, out, acc):
    acc[...] = own_grads[...]
    acc[rows(TILES, TILES), :] += from_next[rows(NAMED, TILES), :].astype(F32)
    acc[rows(0, TILES), :] += from_prev[rows(0, TILES), :].astype(F32)
    for s in range(NAMED):
        acc[rows(slots[0, s]), :] += from_next[rows(s), :].astype(F32)
        acc[rows(TILES + slots[1, s]), :] += from_prev[rows(TILES + s), :].astype(F32)
    out[:, :HD] = dq[...]
    out[:, HD:] = acc[...].astype(BF16)


def columns_of(width, height):
    return pl.BlockSpec((height, width), lambda h, *_: (0, h))


def call(kernel, scalars, ins, outs, scratch, heads, flops, name):
    spec = lambda a: columns_of(a.shape[1] // heads, a.shape[0])
    moved = sum(a.size * a.dtype.itemsize for a in (*ins, *outs))
    return pl.pallas_call(
        kernel,
        grid_spec=pltpu.PrefetchScalarGridSpec(
            num_scalar_prefetch=len(scalars),
            grid=(heads,),
            in_specs=[spec(a) for a in ins],
            out_specs=[spec(a) for a in outs],
            scratch_shapes=scratch,
        ),
        out_shape=outs,
        cost_estimate=pl.CostEstimate(flops=flops, bytes_accessed=moved, transcendentals=0),
        name=name,
    )(*scalars, *ins)


def tables(key_lists, live_counts, axes):
    pair_axis, half_axis = axes
    pairs_total = lax.axis_size(pair_axis)
    z = lax.axis_index(pair_axis)
    x = lax.axis_index(half_axis)
    mine = jnp.concatenate([key_lists, live_counts[:, None]], axis=1)
    other = lax.ppermute(mine, half_axis, [(0, 1), (1, 0)])
    pair = jnp.where(x == 0, jnp.concatenate([mine, other]), jnp.concatenate([other, mine]))
    after = lax.ppermute(pair, pair_axis, [(i + 1, i) for i in range(pairs_total - 1)])
    before = lax.ppermute(pair, pair_axis, [(i, i + 1) for i in range(pairs_total - 1)])
    base = z * PAIR
    lists = jnp.stack([after[:TILES], before[TILES:], pair[:TILES], pair[TILES:]])[:, :, :LISTED]
    lists = lists.reshape(4, TILES * LISTED)
    first = base + jnp.array([0, TILES, -PAIR, PAIR + TILES], jnp.int32)
    order = jnp.arange(TILES, dtype=jnp.int32)
    needed = jnp.any(lists[:, :, None] == (first[:, None] + order[None, :])[:, None, :], axis=1)
    earlier = order[None, :] < order[:, None]
    rank = jnp.sum(jnp.where(earlier[None] & needed[:, None, :], 1, 0), axis=2)
    slot = jnp.arange(NAMED, dtype=jnp.int32)
    chosen = needed[:, None, :] & (rank[:, None, :] == slot[None, :, None])
    slots = jnp.sum(jnp.where(chosen, order[None, None, :], 0), axis=2).astype(jnp.int32)[:2]
    rel = pair[:, :LISTED] - base
    pick = lambda table, at: jnp.sum(jnp.where(at[:, :, None] == order, table, 0), axis=2)
    far_left = pick(rank[2], rel + PAIR)
    far_right = EDGE + PAIR + TILES + pick(rank[3], rel - PAIR - TILES)
    places = jnp.where(rel < -TILES, far_left, jnp.where(rel >= PAIR + TILES, far_right, EDGE + rel))
    places = jnp.clip(places, 0, ALL - 1).astype(jnp.int32)
    block = base + jnp.arange(PAIR, dtype=jnp.int32)
    last = pairs_total * PAIR - 1
    info = jnp.stack([pair[:, LISTED], (block > 0).astype(jnp.int32), (block < last).astype(jnp.int32)])
    return slots, places, info


def shards(qkv, grad_out, key_lists, live_counts):
    group = ("cx", "head")
    ways = lax.axis_size("cx") * lax.axis_size("head")
    pairs_total = lax.axis_size("cz")
    up = [(i, i + 1) for i in range(pairs_total - 1)]
    down = [(i + 1, i) for i in range(pairs_total - 1)]
    slots, places, info = tables(key_lists, live_counts, ("cz", "cx"))
    tokens = qkv.shape[0]
    heads = qkv.shape[1] // (3 * HD) // ways // CHUNKS
    split_qkv = qkv.reshape(tokens, ways, CHUNKS, heads * 3 * HD)
    split_grad = grad_out.reshape(tokens, ways, CHUNKS, heads * HD)
    full = tokens * ways
    sds = jax.ShapeDtypeStruct
    edge = sds((EDGE * BLK, heads * 2 * HD), BF16)

    def gathered(part):
        part = lax.all_to_all(part.transpose(1, 0, 2), group, split_axis=0, concat_axis=0, tiled=True)
        return part.reshape(full, part.shape[2])

    owns, gs, lefts, rights = [], [], [], []
    for c in range(CHUNKS):
        own = gathered(split_qkv[:, :, c])
        to_next, to_prev = call(pack_kernel, (slots,), (own,), (edge, edge), [], heads, 0, "pack")
        owns.append(own)
        lefts.append(lax.ppermute(to_next, "cz", up))
        rights.append(lax.ppermute(to_prev, "cz", down))
        gs.append(gathered(split_grad[:, :, c]))
    results = []
    for c in range(CHUNKS):
        outs = (sds((full, heads * HD), BF16), sds((full, heads * 2 * HD), F32), edge, edge)
        scratch = [pltpu.VMEM((ALL * BLK, 2 * HD), BF16), pltpu.VMEM((ALL * BLK, 2 * HD), F32)]
        flops = heads * PAIR * 5 * 2 * BLK * 7 * BLK * HD
        dq, own_grads, left_grads, right_grads = call(
            attention_kernel, (places, info), (owns[c], gs[c], lefts[c], rights[c]), outs, scratch, heads, flops, "attention"
        )
        from_next = lax.ppermute(left_grads, "cz", down)
        from_prev = lax.ppermute(right_grads, "cz", up)
        (joined,) = call(
            combine_kernel, (slots,), (dq, own_grads, from_next, from_prev), (sds((full, heads * 3 * HD), BF16),),
            [pltpu.VMEM((PAIR * BLK, 2 * HD), F32)], heads, 0, "combine",
        )
        joined = joined.reshape(ways, tokens, heads * 3 * HD)
        results.append(lax.all_to_all(joined, group, split_axis=0, concat_axis=0, tiled=True))
    return jnp.stack(results, axis=1).transpose(2, 0, 1, 3).reshape(qkv.shape)


def solution(mesh):
    ctx, head = mesh.shape["ctx"], mesh.shape["head"]
    split = Mesh(mesh.devices.reshape(ctx // 2, 2, head), ("cz", "cx", "head"))
    both = ("cz", "cx")
    tokens = P((*both, "head"), None)
    return jax.shard_map(
        shards, mesh=split, in_specs=(tokens, tokens, P(both, None), P(both)), out_specs=tokens, check_vma=False
    )
```

```python
import functools

import jax
import jax.numpy as jnp
from jax import lax
from jax.experimental import pallas as pl
from jax.experimental.pallas import tpu as pltpu
from jax.sharding import Mesh, PartitionSpec as P

HD = 128
BLK = 128
TILES = 4
LISTED = 4
NAMED = 2
PAIR = 2 * TILES
EDGE = NAMED + TILES
ALL = 2 * EDGE + PAIR
SCALE = HD ** (-0.5)
MESH = pl.DeviceIdType.MESH
TOGETHER = 2
F32 = jnp.float32
BF16 = jnp.bfloat16


def rows(block, count=1):
    start = block * BLK
    return pl.ds(start if isinstance(start, int) else pl.multiple_of(start, BLK), count * BLK)


def position(sizes):
    pairs_total, heads_total, ways = sizes
    z = lax.axis_index("cz")
    me = lax.axis_index("cx") * heads_total + lax.axis_index("head")
    return z, me


def peer_id(peer, sizes):
    return {"cx": peer // sizes[1], "head": peer % sizes[1]}


def greet(sizes):
    pairs_total, _, ways = sizes
    z, me = position(sizes)
    barrier = pltpu.get_barrier_semaphore()

    def signal(device_id):
        pl.semaphore_signal(barrier, inc=1, device_id=device_id, device_id_type=MESH)

    for k in range(1, ways):
        signal(peer_id((me + k) % ways, sizes))
    pl.when(z > 0)(lambda: signal({"cz": z - 1}))
    pl.when(z < pairs_total - 1)(lambda: signal({"cz": z + 1}))
    pl.semaphore_wait(barrier, ways - 1 + jnp.minimum(z, 1) + jnp.minimum(pairs_total - 1 - z, 1))


def remote(src, dst, send, recv, device_id):
    return pltpu.make_async_remote_copy(
        src_ref=src, dst_ref=dst, send_sem=send, recv_sem=recv, device_id=device_id, device_id_type=MESH
    )


def gather_kernel(sizes, slots, qkv, grads, own, left, right, stage, send, recv, local, edge_send, edge_recv):
    pairs_total, _, ways = sizes
    heads = own.shape[0]
    z, me = position(sizes)
    wide, slim = 3 * HD, HD
    greet(sizes)

    def pieces(h, device, block):
        at = device * heads + h
        return (
            (qkv.at[:, pl.ds(pl.multiple_of(at * wide, HD), wide)], own.at[h, rows(block), pl.ds(0, wide)]),
            (grads.at[:, pl.ds(pl.multiple_of(at * slim, HD), slim)], own.at[h, rows(block), pl.ds(wide, slim)]),
        )

    sends, locals_ = [], []
    for h in range(heads):
        for k in range(1, ways):
            peer = (me + k) % ways
            for t, (src, dst) in enumerate(pieces(h, peer, me)):
                copy = remote(src, dst, send.at[h, k, t], recv.at[h, k, t], peer_id(peer, sizes))
                copy.start()
                sends.append(copy)
        for t, (src, dst) in enumerate(pieces(h, me, me)):
            copy = pltpu.make_async_copy(src, dst, local.at[h, t])
            copy.start()
            locals_.append(copy)

    @pl.when(z == 0)
    def _():
        left[...] = jnp.zeros_like(left)

    @pl.when(z == pairs_total - 1)
    def _():
        right[...] = jnp.zeros_like(right)

    kv = pl.ds(HD, 2 * HD)

    def edge_copies(h):
        up = [
            remote(src, left.at[h, part], edge_send.at[h, 0, n], edge_recv.at[h, 0, n], {"cz": z + 1})
            for n, (src, part) in enumerate(
                ((stage.at[h, 0], rows(0, NAMED)), (own.at[h, rows(TILES, TILES), kv], rows(NAMED, TILES)))
            )
        ]
        down = [
            remote(src, right.at[h, part], edge_send.at[h, 1, n], edge_recv.at[h, 1, n], {"cz": z - 1})
            for n, (src, part) in enumerate(
                ((stage.at[h, 1], rows(TILES, NAMED)), (own.at[h, rows(0, TILES), kv], rows(0, TILES)))
            )
        ]
        return up, down

    for h in range(heads):
        for k in range(1, ways):
            source = (me + ways - k) % ways
            for t, (src, dst) in enumerate(pieces(h, source, source)):
                remote(src, dst, send.at[h, k, t], recv.at[h, k, t], peer_id(source, sizes)).wait_recv()
        locals_[2 * h].wait()
        locals_[2 * h + 1].wait()
        for s in range(NAMED):
            for side in range(2):
                chosen = own[h, rows(side * TILES), HD : 3 * HD]
                for t in range(1, TILES):
                    chosen = jnp.where(slots[side, s] == t, own[h, rows(side * TILES + t), HD : 3 * HD], chosen)
                stage[h, side, rows(s), :] = chosen
        up, down = edge_copies(h)
        pl.when(z < pairs_total - 1)(lambda: [c.start() for c in up] and None)
        pl.when(z > 0)(lambda: [c.start() for c in down] and None)
    for h in range(heads):
        up, down = edge_copies(h)
        pl.when(z > 0)(lambda: [c.wait_recv() for c in up] and None)
        pl.when(z < pairs_total - 1)(lambda: [c.wait_recv() for c in down] and None)
        pl.when(z < pairs_total - 1)(lambda: [c.wait_send() for c in up] and None)
        pl.when(z > 0)(lambda: [c.wait_send() for c in down] and None)
    for copy in sends:
        copy.wait_send()


def return_kernel(
    sizes, slots, dq, own_grads, left_grads, right_grads, out,
    from_next, from_prev, joined, send, recv, local, edge_send, edge_recv,
):
    pairs_total, _, ways = sizes
    heads = dq.shape[0]
    z, me = position(sizes)
    wide = 3 * HD
    greet(sizes)

    @pl.when(z == 0)
    def _():
        from_prev[...] = jnp.zeros_like(from_prev)

    @pl.when(z == pairs_total - 1)
    def _():
        from_next[...] = jnp.zeros_like(from_next)

    def edge_copies(h):
        return (
            remote(right_grads.at[h], from_prev.at[h], edge_send.at[h, 0], edge_recv.at[h, 0], {"cz": z + 1}),
            remote(left_grads.at[h], from_next.at[h], edge_send.at[h, 1], edge_recv.at[h, 1], {"cz": z - 1}),
        )

    def columns(device, h):
        return out.at[:, pl.ds(pl.multiple_of((device * heads + h) * wide, HD), wide)]

    for h in range(heads):
        up, down = edge_copies(h)
        pl.when(z < pairs_total - 1)(up.start)
        pl.when(z > 0)(down.start)
    sends, locals_ = [], []
    for h in range(heads):
        up, down = edge_copies(h)
        pl.when(z > 0)(up.wait_recv)
        pl.when(z < pairs_total - 1)(down.wait_recv)
        for t in range(PAIR):
            total = own_grads[h, rows(t), :]
            if t < TILES:
                near, far, table, base = from_prev, from_next, 0, t
                near_at, far_at = t, 0
            else:
                near, far, table, base = from_next, from_prev, 1, t - TILES
                near_at, far_at = NAMED + t - TILES, TILES
            total += near[h, rows(near_at), :].astype(F32)
            for s in range(NAMED):
                term = far[h, rows(far_at + s), :].astype(F32)
                total += jnp.where(slots[table, s] == base, term, 0.0)
            joined[h, rows(t), pl.ds(HD, 2 * HD)] = total.astype(BF16)
        joined[h, :, pl.ds(0, HD)] = dq[h]
        for k in range(1, ways):
            peer = (me + k) % ways
            copy = remote(joined.at[h, rows(peer)], columns(me, h), send.at[h, k], recv.at[h, k], peer_id(peer, sizes))
            copy.start()
            sends.append(copy)
        copy = pltpu.make_async_copy(joined.at[h, rows(me)], columns(me, h), local.at[h])
        copy.start()
        locals_.append(copy)
    for h in range(heads):
        for k in range(1, ways):
            source = (me + ways - k) % ways
            remote(
                joined.at[h, rows(source)], columns(source, h), send.at[h, k], recv.at[h, k], peer_id(source, sizes)
            ).wait_recv()
        locals_[h].wait()
        up, down = edge_copies(h)
        pl.when(z < pairs_total - 1)(up.wait_send)
        pl.when(z > 0)(down.wait_send)
    for copy in sends:
        copy.wait_send()


def attention_kernel(places, info, own, left, right, dq, own_grads, left_grads, right_grads, pairs, acc):
    pairs[rows(0, EDGE), :] = left[...]
    pairs[rows(EDGE, PAIR), :] = own[:, HD : 3 * HD]
    pairs[rows(EDGE + PAIR, EDGE), :] = right[...]
    acc[...] = jnp.zeros_like(acc)

    def terms_of(i):
        q = own[rows(i), :HD]
        g = own[rows(i), 3 * HD :]
        zero = jnp.zeros_like(q)
        both = jnp.concatenate(
            [jnp.concatenate([q, zero], axis=1), jnp.concatenate([zero, g], axis=1)], axis=0
        )
        where = [EDGE - 1 + i + n for n in range(3)] + [places[i, j] for j in range(LISTED)]
        live = info[0, i]
        usable = [info[1, i] > 0, None, info[2, i] > 0] + [live > j for j in range(LISTED)]
        kv = jnp.concatenate([pairs[rows(p), :] for p in where], axis=0)
        products = lax.dot_general(kv, both, (((1,), (1,)), ((), ())), preferred_element_type=F32)
        scores = []
        for n, ok in enumerate(usable):
            s = products[n * BLK : (n + 1) * BLK, :HD] * SCALE
            scores.append(s if ok is None else jnp.where(ok, s, -1e30))
        scores = jnp.concatenate(scores, axis=0)
        powers = jnp.exp(scores - jnp.max(scores, axis=0, keepdims=True))
        soft = powers * (1.0 / jnp.sum(powers, axis=0, keepdims=True))
        dp = products[:, HD:]
        ds = soft * (dp - jnp.sum(soft * dp, axis=0, keepdims=True))
        ds_low = ds.astype(BF16)
        low = jnp.concatenate([ds_low, soft.astype(BF16)], axis=1)
        terms = jnp.dot(low, both, preferred_element_type=F32)
        grad_q = lax.dot_general(ds_low, kv[:, :HD], (((0,), (0,)), ((), ())), preferred_element_type=F32)
        return where, terms, grad_q

    def step(n, carry):
        blocks = [n * TOGETHER + u for u in range(TOGETHER)]
        found = [terms_of(i) for i in blocks]
        for i, (where, terms, grad_q) in zip(blocks, found):
            dq[rows(i), :] = (grad_q * SCALE).astype(BF16)
            acc[rows(EDGE - 1 + i, 3), :] += terms[: 3 * BLK]
            for j in range(LISTED):
                acc[rows(where[3 + j]), :] += terms[(3 + j) * BLK : (4 + j) * BLK]
        return carry

    lax.fori_loop(0, PAIR // TOGETHER, step, 0)
    for k, factor in ((0, SCALE), (HD, 1.0)):
        columns = slice(k, k + HD)
        own_grads[:, columns] = acc[rows(EDGE, PAIR), columns] * factor
        left_grads[:, columns] = (acc[rows(0, EDGE), columns] * factor).astype(BF16)
        right_grads[:, columns] = (acc[rows(EDGE + PAIR, EDGE), columns] * factor).astype(BF16)


def tables(key_lists, live_counts, axes):
    pair_axis, half_axis = axes
    pairs_total = lax.axis_size(pair_axis)
    z = lax.axis_index(pair_axis)
    x = lax.axis_index(half_axis)
    mine = jnp.concatenate([key_lists, live_counts[:, None]], axis=1)
    other = lax.ppermute(mine, half_axis, [(0, 1), (1, 0)])
    pair = jnp.where(x == 0, jnp.concatenate([mine, other]), jnp.concatenate([other, mine]))
    after = lax.ppermute(pair, pair_axis, [(i + 1, i) for i in range(pairs_total - 1)])
    before = lax.ppermute(pair, pair_axis, [(i, i + 1) for i in range(pairs_total - 1)])
    base = z * PAIR
    lists = jnp.stack([after[:TILES], before[TILES:], pair[:TILES], pair[TILES:]])[:, :, :LISTED]
    lists = lists.reshape(4, TILES * LISTED)
    first = base + jnp.array([0, TILES, -PAIR, PAIR + TILES], jnp.int32)
    order = jnp.arange(TILES, dtype=jnp.int32)
    needed = jnp.any(lists[:, :, None] == (first[:, None] + order[None, :])[:, None, :], axis=1)
    earlier = order[None, :] < order[:, None]
    rank = jnp.sum(jnp.where(earlier[None] & needed[:, None, :], 1, 0), axis=2)
    slot = jnp.arange(NAMED, dtype=jnp.int32)
    chosen = needed[:, None, :] & (rank[:, None, :] == slot[None, :, None])
    slots = jnp.sum(jnp.where(chosen, order[None, None, :], 0), axis=2).astype(jnp.int32)[:2]
    rel = pair[:, :LISTED] - base
    pick = lambda table, at: jnp.sum(jnp.where(at[:, :, None] == order, table, 0), axis=2)
    far_left = pick(rank[2], rel + PAIR)
    far_right = EDGE + PAIR + TILES + pick(rank[3], rel - PAIR - TILES)
    places = jnp.where(rel < -TILES, far_left, jnp.where(rel >= PAIR + TILES, far_right, EDGE + rel))
    places = jnp.clip(places, 0, ALL - 1).astype(jnp.int32)
    block = base + jnp.arange(PAIR, dtype=jnp.int32)
    last = pairs_total * PAIR - 1
    info = jnp.stack([pair[:, LISTED], (block > 0).astype(jnp.int32), (block < last).astype(jnp.int32)])
    return slots, places, info


def shards(qkv, grad_out, key_lists, live_counts):
    heads_total = lax.axis_size("head")
    ways = lax.axis_size("cx") * heads_total
    sizes = (lax.axis_size("cz"), heads_total, ways)
    slots, places, info = tables(key_lists, live_counts, ("cz", "cx"))
    heads = qkv.shape[1] // (3 * HD) // ways
    full = qkv.shape[0] * ways
    sds = jax.ShapeDtypeStruct
    edge = sds((heads, EDGE * BLK, 2 * HD), BF16)
    vmem = pl.BlockSpec(memory_space=pltpu.VMEM)
    smem = pl.BlockSpec(memory_space=pltpu.SMEM)
    anywhere = pl.BlockSpec(memory_space=pl.ANY)
    dma = pltpu.SemaphoreType.DMA
    own, left, right = pl.pallas_call(
        functools.partial(gather_kernel, sizes),
        in_specs=[smem, anywhere, anywhere],
        out_specs=[vmem] * 3,
        out_shape=(sds((heads, full, 4 * HD), BF16), edge, edge),
        scratch_shapes=[
            pltpu.VMEM((heads, 2, NAMED * BLK, 2 * HD), BF16),
            dma((heads, ways, 2)), dma((heads, ways, 2)), dma((heads, 2)), dma((heads, 2, 2)), dma((heads, 2, 2)),
        ],
        compiler_params=pltpu.CompilerParams(collective_id=0, has_side_effects=True),
        name="gather",
    )(slots, qkv, grad_out)
    block = lambda a: pl.BlockSpec((None, *a.shape[1:]), lambda h, *_: (h, 0, 0))
    outs = (sds((heads, full, HD), BF16), sds((heads, full, 2 * HD), F32), edge, edge)
    grads = pl.pallas_call(
        attention_kernel,
        grid_spec=pltpu.PrefetchScalarGridSpec(
            num_scalar_prefetch=2,
            grid=(heads,),
            in_specs=[block(a) for a in (own, left, right)],
            out_specs=[block(a) for a in outs],
            scratch_shapes=[pltpu.VMEM((ALL * BLK, 2 * HD), BF16), pltpu.VMEM((ALL * BLK, 2 * HD), F32)],
        ),
        out_shape=outs,
        name="attention",
    )(places, info, own, left, right)
    return pl.pallas_call(
        functools.partial(return_kernel, sizes),
        in_specs=[smem, vmem, vmem, anywhere, anywhere],
        out_specs=anywhere,
        out_shape=sds(qkv.shape, BF16),
        scratch_shapes=[
            pltpu.VMEM(edge.shape, BF16), pltpu.VMEM(edge.shape, BF16), pltpu.VMEM((heads, full, 3 * HD), BF16),
            dma((heads, ways)), dma((heads, ways)), dma((heads,)), dma((heads, 2)), dma((heads, 2)),
        ],
        compiler_params=pltpu.CompilerParams(collective_id=1, has_side_effects=True),
        name="give_back",
    )(slots, *grads)


def solution(mesh):
    ctx, head = mesh.shape["ctx"], mesh.shape["head"]
    split = Mesh(mesh.devices.reshape(ctx // 2, 2, head), ("cz", "cx", "head"))
    both = ("cz", "cx")
    tokens = P((*both, "head"), None)
    return jax.shard_map(
        shards, mesh=split, in_specs=(tokens, tokens, P(both, None), P(both)), out_specs=tokens, check_vma=False
    )
```
